32 devices in a mesh: groups: 2 (over y), row: 4 (over z), col: 2 (over x), aux: 2 (over core).
Axes of the slice: x: 2, y: 2, z: 4, core: 2. Of those that a mesh axis runs over, the one named last changes fastest.
Arguments:
- amplitudes: bfloat16 [32768, 16384], P(('groups', 'row'), ('col', 'aux')), parts along dimension 0, may hold values from -6 to 6, as said below
- b_factors: bfloat16 [32768, 512], P(('groups', 'row'), ('col', 'aux')), parts along dimension 0, may hold values from -0.25 to 0.25
- fock_blocks: bfloat16 [32768, 256], P(('groups', 'row')), parts along dimension 0, may hold values from -0.375 to 0.375
- occ_index: int32 [32768], P('groups'), parts along dimension 0, may hold values from 0 to 63, as said below
- virt_index: int32 [32768], P('groups'), parts along dimension 0, may hold values from 0 to 255, as said below
- eps_occ: float32 [128], P('groups'), parts along dimension 0, may hold values from -3 to -0.5
- eps_virt: float32 [512], P('groups'), parts along dimension 0, may hold values from 0.5 to 3
Outputs:
- t_next: bfloat16 [32768, 16384], P(('groups', 'row'), ('col', 'aux')), parts along dimension 0
The draws below stay inside these ranges and needn't reach their ends.
There are 2 independent parts, one for each index of `groups`. The reference program is written for one: setup_inputs(seed, part) draws one part's arguments, and reference() takes and returns one part's arrays. A program takes and returns all parts, laid end to end along the dimension named above; each array names one. Nothing has to cross between parts.
Inputs may be any that keep to these rules, and one draw needn't show every extreme that they name: amplitudes is symmetric: amplitudes[p, q] == amplitudes[q, p]. `occ_index`: pairs are occupied-major: all pairs of diagonal block k (p // 256 == k) share one occupied orbital, and distinct blocks have distinct ones. `virt_index`: within each diagonal block the 256 pairs have distinct virtual orbitals, in the same order for every block.
All inputs are finite; a program needn't handle non-finite values.
Results may differ from the reference program's by a relative error of at most 0.0023.
Values may be sent and summed in bfloat16 or wider, within the bound.
A program may use at most 512 MiB of HBM per device.

```python
import jax
import jax.numpy as jnp

NOCC = 64
NVIRT = 256
NAUX = 512
P_SIZE = 16384


def draw_amplitudes(key, part):
    base = jnp.clip(jax.random.normal(key, (P_SIZE, P_SIZE), jnp.float32), -4.0, 4.0)
    return ((base + base.T) * 0.7071).astype(jnp.bfloat16)


def draw_occ_index(key, part):
    labels = jax.random.permutation(jax.random.fold_in(key, 11), NOCC).astype(jnp.int32)
    return jnp.repeat(labels, NVIRT)


def draw_virt_index(key, part):
    labels = jax.random.permutation(jax.random.fold_in(key, 23), NVIRT).astype(jnp.int32)
    return jnp.tile(labels, NOCC)


def levels(key, shape, shards, least, largest):
    factor_of = 1.0
    for position, shards_of in shards:
        draws = jax.random.uniform(jax.random.fold_in(jax.random.fold_in(key, 6), position), (shards_of,), jnp.float32, least / len(shards), largest / len(shards))
        factor_of = factor_of * jnp.repeat(jnp.exp(draws), shape[position] // shards_of).reshape((-1,) + (1,) * (len(shape) - 1 - position))
    return factor_of


def scatter_about(stream_key, shape, deviation, reach, split=(), kind=jnp.bfloat16):
    result = jax.random.normal(stream_key, shape, jnp.float32) * deviation
    if len(split) > 0:
        result = levels(stream_key, shape, split, -0.22, 0.18) * result
    return jnp.clip(result, min=-reach, max=reach).astype(kind)


def setup_inputs(seed: int = 0, part: int = 0) -> dict:
    streams_of = jax.random.split(jax.random.key(seed), 8)
    own_keys = jax.random.split(jax.random.fold_in(streams_of[7], part), 8)
    return {
        "amplitudes": draw_amplitudes(jax.random.fold_in(jax.random.fold_in(streams_of[7], part), 71), part),
        "b_factors": scatter_about(own_keys[1], (P_SIZE, NAUX), ((P_SIZE * NAUX) ** -0.25), 0.25, ((0, 4), (1, 4))),
        "fock_blocks": scatter_about(own_keys[2], (P_SIZE, NVIRT), NVIRT ** -0.5, 0.375, ((0, 4),)),
        "occ_index": draw_occ_index(jax.random.fold_in(jax.random.fold_in(streams_of[7], part), 71), part),
        "virt_index": draw_virt_index(jax.random.fold_in(jax.random.fold_in(streams_of[7], part), 71), part),
        "eps_occ": jnp.clip(jax.random.uniform(own_keys[5], (NOCC,), jnp.float32, -3.0, -0.5), -3.0, -0.5),
        "eps_virt": jnp.clip(jax.random.uniform(own_keys[6], (NVIRT,), jnp.float32, 0.5, 3.0), 0.5, 3.0),
    }


def reference(amplitudes, b_factors, fock_blocks, occ_index, virt_index, eps_occ, eps_virt):
    gmat = jnp.dot(amplitudes, b_factors, preferred_element_type=jnp.float32).astype(jnp.bfloat16)
    blocks = P_SIZE // NVIRT
    tshaped = amplitudes.astype(jnp.float32).reshape(P_SIZE, blocks, NVIRT)
    dshaped = fock_blocks.astype(jnp.float32).reshape(blocks, NVIRT, NVIRT)
    tdprod = jnp.einsum("xkd,kde->xke", tshaped, dshaped).reshape(P_SIZE, P_SIZE)
    zmat = jnp.dot(gmat, b_factors.T, preferred_element_type=jnp.float32) + tdprod
    resmat = zmat + zmat.T
    energy = eps_virt[virt_index] - eps_occ[occ_index]
    delta = energy[:, None] + energy[None, :]
    return (amplitudes.astype(jnp.float32) - resmat / delta).astype(jnp.bfloat16)
```

```python
import functools

import jax
import jax.numpy as jnp
from jax import lax
from jax.experimental import pallas as pl
from jax.experimental.pallas import tpu as pltpu
from jax.sharding import PartitionSpec as P

MESH = pl.DeviceIdType.MESH
LANES = 128
ROW_TILE = 512
COL_TILE = 512
VMEM_BYTES = 60 * 1024 * 1024


def pair_energy(occ_part, virt_part, eps_occ, eps_virt):
    virt_hit = virt_part[:, None] == jnp.arange(eps_virt.shape[0], dtype=jnp.int32)[None, :]
    occ_hit = occ_part[:, None] == jnp.arange(eps_occ.shape[0], dtype=jnp.int32)[None, :]
    upper = jnp.sum(jnp.where(virt_hit, eps_virt[None, :], 0.0), axis=1)
    lower = jnp.sum(jnp.where(occ_hit, eps_occ[None, :], 0.0), axis=1)
    return upper - lower


def slab(ref, index, width, start, size):
    if width % LANES == 0:
        return ref.at[pl.ds(start, size), pl.ds(pl.multiple_of(index * width, LANES), width)]
    return ref.at[index, pl.ds(start, size)]


def slab_shape(count, rows, width):
    return (rows, count * width) if width % LANES == 0 else (count, rows, width)


def whole(array):
    if array.ndim == 2:
        return array
    count, rows, width = array.shape
    return array.transpose(1, 0, 2).reshape(rows, count * width)


def meet(row, col, aux, rows, cols, auxs):
    barrier = pltpu.get_barrier_semaphore()

    def greet(device):
        pl.semaphore_signal(barrier, inc=1, device_id=device, device_id_type=MESH)

    @pl.when(row > 0)
    def _():
        greet({"row": row - 1})

    @pl.when(row < rows - 1)
    def _():
        greet({"row": row + 1})

    for step in range(1, cols * auxs):
        other = lax.rem(col * auxs + aux + step, cols * auxs)
        greet({"col": other // auxs, "aux": lax.rem(other, auxs)})
    above = jnp.where(row > 0, 1, 0)
    below = jnp.where(row < rows - 1, 1, 0)
    pl.semaphore_wait(barrier, cols * auxs - 1 + above + below)


def exchange_kernel(
    rows, cols, auxs, pieces, loc, along, mine, other,
    zsend, zrecv, csend, crecv, rsend, rrecv, lsem,
):
    row, col, aux = lax.axis_index("row"), lax.axis_index("col"), lax.axis_index("aux")
    count = cols * auxs
    me = col * auxs + aux
    height, width = loc.shape
    size = height // pieces
    meet(row, col, aux, rows, cols, auxs)

    def held(k, p, own):
        return loc.at[pl.ds(p * size, size)] if own else along.at[k, pl.ds(p * size, size)]

    def z_copy(k, p, step, own=False):
        return pltpu.make_async_remote_copy(
            src_ref=held(k, p, own),
            dst_ref=along.at[k, pl.ds(p * size, size)],
            send_sem=zsend.at[(1 - step) // 2, k, p],
            recv_sem=zrecv.at[k, p],
            device_id={"row": row + step},
            device_id_type=MESH,
        )

    def c_copy(k, p, slot, own=False):
        return pltpu.make_async_remote_copy(
            src_ref=held(k, p, own),
            dst_ref=slab(other, slot, width, p * size, size),
            send_sem=csend.at[k, p],
            recv_sem=crecv.at[slot, p],
            device_id={"col": k // auxs, "aux": lax.rem(k, auxs)},
            device_id_type=MESH,
        )

    def c_local(k, p, own=False):
        return pltpu.make_async_copy(
            held(k, p, own), slab(other, me, width, p * size, size), lsem.at[1 + p]
        )

    def dispatch(k, p, own=False):
        @pl.when(k != me)
        def _():
            c_copy(k, p, me, own).start()

        @pl.when(k == me)
        def _():
            c_local(k, p, own).start()

    def r_copy(index, to_col, to_aux, hop, own):
        return pltpu.make_async_remote_copy(
            src_ref=loc if own else slab(mine, index, width, 0, height),
            dst_ref=slab(mine, index, width, 0, height),
            send_sem=rsend.at[hop],
            recv_sem=rrecv.at[index],
            device_id={"col": to_col, "aux": to_aux},
            device_id_type=MESH,
        )

    def r_sends():
        first, second = [], []
        for step in range(1, cols):
            first.append(r_copy(me, lax.rem(col + step, cols), aux, step - 1, True))
        hop = cols - 1
        for step in range(cols):
            from_col = lax.rem(col + step, cols)
            for turn in range(1, auxs):
                second.append((
                    from_col * auxs + aux,
                    r_copy(from_col * auxs + aux, col, lax.rem(aux + turn, auxs), hop, step == 0),
                ))
                hop += 1
        return first, second

    first, second = r_sends()
    for copy in first:
        copy.start()
    for _, copy in second[: auxs - 1]:
        copy.start()
    for p in range(pieces):
        @pl.when(row < rows - 1)
        def _(p=p):
            z_copy(row, p, 1, True).start()

        @pl.when(row > 0)
        def _(p=p):
            z_copy(row, p, -1, True).start()

        dispatch(row, p, True)
    local = pltpu.make_async_copy(loc, slab(mine, me, width, 0, height), lsem.at[0])
    local.start()

    for s in range(1, rows):
        for p in range(pieces):
            @pl.when(row - s >= 0)
            def _(s=s, p=p):
                k = row - s
                z_copy(k, p, 1).wait_recv()

                @pl.when(row < rows - 1)
                def _():
                    z_copy(k, p, 1).start()

                dispatch(k, p)

            @pl.when(row + s < rows)
            def _(s=s, p=p):
                k = row + s
                z_copy(k, p, -1).wait_recv()

                @pl.when(row > 0)
                def _():
                    z_copy(k, p, -1).start()

                dispatch(k, p)
        if s == 1:
            for index, copy in second[auxs - 1:]:
                r_copy(index, col, aux, 0, False).wait_recv()
                copy.start()

    for step in range(cols):
        from_col = lax.rem(col + step, cols)
        for turn in range(1, auxs):
            index = from_col * auxs + lax.rem(aux + turn, auxs)
            r_copy(index, col, aux, 0, False).wait_recv()
    for copy in first:
        copy.wait_send()
    for _, copy in second:
        copy.wait_send()
    local.wait()
    for step in range(1, count):
        index = lax.rem(me + step, count)
        for p in range(pieces):
            c_copy(me, p, index).wait_recv()
    for k in range(rows):
        for p in range(pieces):
            @pl.when(k != me)
            def _(k=k, p=p):
                c_copy(k, p, me).wait_send()

            @pl.when(k == me)
            def _(k=k, p=p):
                c_local(k, p).wait()

            @pl.when((row < rows - 1) & (row >= k))
            def _(k=k, p=p):
                z_copy(k, p, 1).wait_send()

            @pl.when((row > 0) & (row <= k))
            def _(k=k, p=p):
                z_copy(k, p, -1).wait_send()


def exchange(loc, sizes, collective_id):
    rows, cols, auxs = sizes
    count = cols * auxs
    height, width = loc.shape
    pieces = max(1, 16 // rows)
    shape = slab_shape(count, height, width)
    hops = cols - 1 + cols * (auxs - 1)
    any_space = pl.BlockSpec(memory_space=pl.ANY)
    _, mine, other = pl.pallas_call(
        functools.partial(exchange_kernel, rows, cols, auxs, pieces),
        out_shape=(
            jax.ShapeDtypeStruct((rows, height, width), loc.dtype),
            jax.ShapeDtypeStruct(shape, loc.dtype),
            jax.ShapeDtypeStruct(shape, loc.dtype),
        ),
        in_specs=[any_space],
        out_specs=(any_space, any_space, any_space),
        scratch_shapes=[
            pltpu.SemaphoreType.DMA((2, rows, pieces)),
            pltpu.SemaphoreType.DMA((rows, pieces)),
            pltpu.SemaphoreType.DMA((rows, pieces)),
            pltpu.SemaphoreType.DMA((count, pieces)),
            pltpu.SemaphoreType.DMA((hops,)),
            pltpu.SemaphoreType.DMA((count,)),
            pltpu.SemaphoreType.DMA((1 + pieces,)),
        ],
        compiler_params=pltpu.CompilerParams(
            collective_id=collective_id, has_side_effects=True
        ),
        name="exchange%d" % collective_id,
    )(loc)
    return whole(mine), whole(other)


def reduce_kernel(
    rows, cols, auxs, pieces, part, fock, total, diag, landed,
    psend, precv, dsend, drecv, lsem,
):
    row, col, aux = lax.axis_index("row"), lax.axis_index("col"), lax.axis_index("aux")
    count = cols * auxs
    me = col * auxs + aux
    height, width = total.shape
    size = height // pieces
    meet(row, col, aux, rows, cols, auxs)

    def p_copy(index, slot):
        return pltpu.make_async_remote_copy(
            src_ref=slab(part, index, width, 0, height),
            dst_ref=landed.at[slot],
            send_sem=psend.at[index],
            recv_sem=precv.at[slot],
            device_id={"col": index // auxs, "aux": lax.rem(index, auxs)},
            device_id_type=MESH,
        )

    def d_copy(p, step, own):
        piece = pl.ds(p * size, size)
        return pltpu.make_async_remote_copy(
            src_ref=fock.at[piece] if own else diag.at[piece],
            dst_ref=diag.at[piece],
            send_sem=dsend.at[(1 - step) // 2, p],
            recv_sem=drecv.at[p],
            device_id={"row": row + step},
            device_id_type=MESH,
        )

    for step in range(1, count):
        p_copy(lax.rem(me + step, count), me).start()
    own_part = pltpu.make_async_copy(
        slab(part, me, width, 0, height), landed.at[me], lsem.at[0]
    )
    own_part.start()
    own_diag = pltpu.make_async_copy(fock, diag, lsem.at[1])

    @pl.when(row == me)
    def _():
        own_diag.start()

    up, down = row < rows - 1, row > 0
    for p in range(pieces):
        @pl.when((row == me) & up)
        def _(p=p):
            d_copy(p, 1, True).start()

        @pl.when((row == me) & down)
        def _(p=p):
            d_copy(p, -1, True).start()

        @pl.when(row > me)
        def _(p=p):
            d_copy(p, 1, False).wait_recv()

            @pl.when(up)
            def _():
                d_copy(p, 1, False).start()

        @pl.when(row < me)
        def _(p=p):
            d_copy(p, -1, False).wait_recv()

            @pl.when(down)
            def _():
                d_copy(p, -1, False).start()

    own_part.wait()
    for step in range(1, count):
        p_copy(me, lax.rem(me + step, count)).wait_recv()

    tile = 256

    @pl.loop(0, height // tile)
    def _(i):
        at = pl.ds(pl.multiple_of(i * tile, tile), tile)
        acc = landed[0, at, :].astype(jnp.float32)
        for index in range(1, count):
            acc = acc + landed[index, at, :].astype(jnp.float32)
        total[at, :] = acc.astype(total.dtype)

    for step in range(1, count):
        p_copy(lax.rem(me + step, count), me).wait_send()

    @pl.when(row == me)
    def _():
        own_diag.wait()

    for p in range(pieces):
        @pl.when(up & (row >= me))
        def _(p=p):
            d_copy(p, 1, False).wait_send()

        @pl.when(down & (row <= me))
        def _(p=p):
            d_copy(p, -1, False).wait_send()


def reduce_rows(part, fock, sizes, collective_id):
    rows, cols, auxs = sizes
    count = cols * auxs
    height, virt = fock.shape
    width = part.shape[1] // count
    pieces = 4
    if width % LANES:
        part = part.reshape(height, count, width).transpose(1, 0, 2)
    any_space = pl.BlockSpec(memory_space=pl.ANY)
    return pl.pallas_call(
        functools.partial(reduce_kernel, rows, cols, auxs, pieces),
        out_shape=(
            jax.ShapeDtypeStruct((height, width), part.dtype),
            jax.ShapeDtypeStruct((height, virt), fock.dtype),
        ),
        in_specs=[any_space, any_space],
        out_specs=(pl.BlockSpec(memory_space=pltpu.VMEM), any_space),
        scratch_shapes=[
            pltpu.VMEM((count, height, width), part.dtype),
            pltpu.SemaphoreType.DMA((count,)),
            pltpu.SemaphoreType.DMA((count,)),
            pltpu.SemaphoreType.DMA((2, pieces)),
            pltpu.SemaphoreType.DMA((pieces,)),
            pltpu.SemaphoreType.DMA((2,)),
        ],
        compiler_params=pltpu.CompilerParams(
            collective_id=collective_id, has_side_effects=True, vmem_limit_bytes=VMEM_BYTES
        ),
        name="reduce%d" % collective_id,
    )(part, fock)


def update_kernel(
    virt, tile, t_ref, g_row, b_row, f_row, e_row, g_col, b_col, f_col, e_col, out
):
    high, across = t_ref.shape
    contract = (((1,), (1,)), ((), ()))

    @pl.loop(0, across // tile)
    def _(j):
        base = pl.multiple_of(j * tile, tile)
        at = pl.ds(base, tile)
        acc = lax.dot_general(
            g_row[...], b_col[at, :], contract, preferred_element_type=jnp.float32
        )
        acc = acc + lax.dot_general(
            b_row[...], g_col[at, :], contract, preferred_element_type=jnp.float32
        )
        right = [
            jnp.dot(
                t_ref[:, pl.ds(pl.multiple_of(base + k * virt, virt), virt)],
                f_col[pl.ds(pl.multiple_of(base + k * virt, virt), virt), :],
                preferred_element_type=jnp.float32,
            )
            for k in range(tile // virt)
        ]
        left = [
            lax.dot_general(
                f_row[k * virt:(k + 1) * virt, :],
                t_ref[k * virt:(k + 1) * virt, at],
                (((0,), (0,)), ((), ())),
                preferred_element_type=jnp.float32,
            )
            for k in range(high // virt)
        ]
        acc = acc + jnp.concatenate(right, axis=1) + jnp.concatenate(left, axis=0)
        delta = e_row[...] + e_col[:, at]
        out[:, at] = (t_ref[:, at].astype(jnp.float32) - acc / delta).astype(out.dtype)


def update(amplitudes, g_rows, b_rows, fock, e_rows, g_cols, b_cols, diag, e_cols):
    high, across = amplitudes.shape
    virt = fock.shape[1]
    aux = b_rows.shape[1]
    row_tile, col_tile = min(ROW_TILE, high), min(COL_TILE, across)
    by_row = lambda i: (i, 0)
    fixed = lambda i: (0, 0)
    return pl.pallas_call(
        functools.partial(update_kernel, virt, col_tile),
        out_shape=jax.ShapeDtypeStruct(amplitudes.shape, amplitudes.dtype),
        grid=(high // row_tile,),
        in_specs=[
            pl.BlockSpec((row_tile, across), by_row),
            pl.BlockSpec((row_tile, aux), by_row),
            pl.BlockSpec((row_tile, aux), by_row),
            pl.BlockSpec((row_tile, virt), by_row),
            pl.BlockSpec((row_tile, 1), by_row),
            pl.BlockSpec((across, aux), fixed),
            pl.BlockSpec((across, aux), fixed),
            pl.BlockSpec((across, virt), fixed),
            pl.BlockSpec((1, across), fixed),
        ],
        out_specs=pl.BlockSpec((row_tile, across), by_row),
        compiler_params=pltpu.CompilerParams(vmem_limit_bytes=VMEM_BYTES),
        name="update",
    )(amplitudes, g_rows, b_rows, fock, e_rows, g_cols, b_cols, diag, e_cols)


def body(sizes, amplitudes, b_factors, fock_blocks, occ_index, virt_index, eps_occ, eps_virt):
    height, across = amplitudes.shape
    b_rows, b_cols = exchange(b_factors, sizes, 0)
    part = jnp.dot(amplitudes, b_cols, preferred_element_type=jnp.float32)
    g_own, diag = reduce_rows(part.astype(jnp.bfloat16), fock_blocks, sizes, 1)
    g_rows, g_cols = exchange(g_own, sizes, 2)

    def energy(start, size):
        return pair_energy(
            lax.dynamic_slice_in_dim(occ_index, start, size),
            lax.dynamic_slice_in_dim(virt_index, start, size),
            eps_occ,
            eps_virt,
        )

    e_rows = energy(lax.axis_index("row") * height, height)
    e_cols = energy(lax.axis_index(("col", "aux")) * across, across)
    return update(
        amplitudes, g_rows, b_rows, fock_blocks, e_rows[:, None],
        g_cols, b_cols, diag, e_cols[None, :],
    )


def solution(mesh):
    in_specs = (
        P(("groups", "row"), ("col", "aux")),
        P(("groups", "row"), ("col", "aux")),
        P(("groups", "row"), None),
        P("groups"),
        P("groups"),
        P("groups"),
        P("groups"),
    )
    out_specs = P(("groups", "row"), ("col", "aux"))
    sizes = (mesh.shape["row"], mesh.shape["col"], mesh.shape["aux"])
    return jax.shard_map(
        functools.partial(body, sizes),
        mesh=mesh, in_specs=in_specs, out_specs=out_specs, check_vma=False,
    )
```

```python
import functools

import jax
import jax.numpy as jnp
from jax import lax
from jax.experimental import pallas as pl
from jax.experimental.pallas import tpu as pltpu
from jax.sharding import PartitionSpec as P

MESH = pl.DeviceIdType.MESH
LANES = 128
ROW_TILE = 512
COL_TILE = 1024
VMEM_BYTES = 60 * 1024 * 1024


def pair_energy(occ_part, virt_part, eps_occ, eps_virt):
    virt_hit = virt_part[:, None] == jnp.arange(eps_virt.shape[0], dtype=jnp.int32)[None, :]
    occ_hit = occ_part[:, None] == jnp.arange(eps_occ.shape[0], dtype=jnp.int32)[None, :]
    upper = jnp.sum(jnp.where(virt_hit, eps_virt[None, :], 0.0), axis=1)
    lower = jnp.sum(jnp.where(occ_hit, eps_occ[None, :], 0.0), axis=1)
    return upper - lower


def slab(ref, index, width, start, size):
    if width % LANES == 0:
        return ref.at[pl.ds(start, size), pl.ds(pl.multiple_of(index * width, LANES), width)]
    return ref.at[index, pl.ds(start, size)]


def slab_shape(count, rows, width):
    return (rows, count * width) if width % LANES == 0 else (count, rows, width)


def whole(array):
    if array.ndim == 2:
        return array
    count, rows, width = array.shape
    return array.transpose(1, 0, 2).reshape(rows, count * width)


def meet(row, col, aux, rows, cols, auxs):
    barrier = pltpu.get_barrier_semaphore()

    def greet(device):
        pl.semaphore_signal(barrier, inc=1, device_id=device, device_id_type=MESH)

    @pl.when(row > 0)
    def _():
        greet({"row": row - 1})

    @pl.when(row < rows - 1)
    def _():
        greet({"row": row + 1})

    for step in range(1, cols * auxs):
        other = lax.rem(col * auxs + aux + step, cols * auxs)
        greet({"col": other // auxs, "aux": lax.rem(other, auxs)})
    above = jnp.where(row > 0, 1, 0)
    below = jnp.where(row < rows - 1, 1, 0)
    pl.semaphore_wait(barrier, cols * auxs - 1 + above + below)


def exchange_kernel(
    rows, cols, auxs, pieces, loc, along, mine, other,
    zsend, zrecv, csend, crecv, rsend, rrecv, lsem,
):
    row, col, aux = lax.axis_index("row"), lax.axis_index("col"), lax.axis_index("aux")
    count = cols * auxs
    me = col * auxs + aux
    height, width = loc.shape
    size = height // pieces
    meet(row, col, aux, rows, cols, auxs)

    def held(k, p, own):
        return loc.at[pl.ds(p * size, size)] if own else along.at[k, pl.ds(p * size, size)]

    def z_copy(k, p, step, own=False):
        return pltpu.make_async_remote_copy(
            src_ref=held(k, p, own),
            dst_ref=along.at[k, pl.ds(p * size, size)],
            send_sem=zsend.at[(1 - step) // 2, k, p],
            recv_sem=zrecv.at[k, p],
            device_id={"row": row + step},
            device_id_type=MESH,
        )

    def c_copy(k, p, slot, own=False):
        return pltpu.make_async_remote_copy(
            src_ref=held(k, p, own),
            dst_ref=slab(other, slot, width, p * size, size),
            send_sem=csend.at[k, p],
            recv_sem=crecv.at[slot, p],
            device_id={"col": k // auxs, "aux": lax.rem(k, auxs)},
            device_id_type=MESH,
        )

    def c_local(k, p, own=False):
        return pltpu.make_async_copy(
            held(k, p, own), slab(other, me, width, p * size, size), lsem.at[1 + p]
        )

    def dispatch(k, p, own=False):
        @pl.when(k != me)
        def _():
            c_copy(k, p, me, own).start()

        @pl.when(k == me)
        def _():
            c_local(k, p, own).start()

    def r_copy(index, to_col, to_aux, hop, own):
        return pltpu.make_async_remote_copy(
            src_ref=loc if own else slab(mine, index, width, 0, height),
            dst_ref=slab(mine, index, width, 0, height),
            send_sem=rsend.at[hop],
            recv_sem=rrecv.at[index],
            device_id={"col": to_col, "aux": to_aux},
            device_id_type=MESH,
        )

    def r_sends():
        first, second = [], []
        for step in range(1, cols):
            first.append(r_copy(me, lax.rem(col + step, cols), aux, step - 1, True))
        hop = cols - 1
        for step in range(cols):
            from_col = lax.rem(col + step, cols)
            for turn in range(1, auxs):
                second.append((
                    from_col * auxs + aux,
                    r_copy(from_col * auxs + aux, col, lax.rem(aux + turn, auxs), hop, step == 0),
                ))
                hop += 1
        return first, second

    first, second = r_sends()
    for copy in first:
        copy.start()
    for _, copy in second[: auxs - 1]:
        copy.start()
    for p in range(pieces):
        @pl.when(row < rows - 1)
        def _(p=p):
            z_copy(row, p, 1, True).start()

        @pl.when(row > 0)
        def _(p=p):
            z_copy(row, p, -1, True).start()

        dispatch(row, p, True)
    local = pltpu.make_async_copy(loc, slab(mine, me, width, 0, height), lsem.at[0])
    local.start()

    for s in range(1, rows):
        for p in range(pieces):
            @pl.when(row - s >= 0)
            def _(s=s, p=p):
                k = row - s
                z_copy(k, p, 1).wait_recv()

                @pl.when(row < rows - 1)
                def _():
                    z_copy(k, p, 1).start()

                dispatch(k, p)

            @pl.when(row + s < rows)
            def _(s=s, p=p):
                k = row + s
                z_copy(k, p, -1).wait_recv()

                @pl.when(row > 0)
                def _():
                    z_copy(k, p, -1).start()

                dispatch(k, p)
        if s == 1:
            for index, copy in second[auxs - 1:]:
                r_copy(index, col, aux, 0, False).wait_recv()
                copy.start()

    for step in range(cols):
        from_col = lax.rem(col + step, cols)
        for turn in range(1, auxs):
            index = from_col * auxs + lax.rem(aux + turn, auxs)
            r_copy(index, col, aux, 0, False).wait_recv()
    for copy in first:
        copy.wait_send()
    for _, copy in second:
        copy.wait_send()
    local.wait()
    for step in range(1, count):
        index = lax.rem(me + step, count)
        for p in range(pieces):
            c_copy(me, p, index).wait_recv()
    for k in range(rows):
        for p in range(pieces):
            @pl.when(k != me)
            def _(k=k, p=p):
                c_copy(k, p, me).wait_send()

            @pl.when(k == me)
            def _(k=k, p=p):
                c_local(k, p).wait()

            @pl.when((row < rows - 1) & (row >= k))
            def _(k=k, p=p):
                z_copy(k, p, 1).wait_send()

            @pl.when((row > 0) & (row <= k))
            def _(k=k, p=p):
                z_copy(k, p, -1).wait_send()


def exchange(loc, sizes, collective_id):
    rows, cols, auxs = sizes
    count = cols * auxs
    height, width = loc.shape
    pieces = max(1, 16 // rows)
    shape = slab_shape(count, height, width)
    hops = cols - 1 + cols * (auxs - 1)
    any_space = pl.BlockSpec(memory_space=pl.ANY)
    _, mine, other = pl.pallas_call(
        functools.partial(exchange_kernel, rows, cols, auxs, pieces),
        out_shape=(
            jax.ShapeDtypeStruct((rows, height, width), loc.dtype),
            jax.ShapeDtypeStruct(shape, loc.dtype),
            jax.ShapeDtypeStruct(shape, loc.dtype),
        ),
        in_specs=[any_space],
        out_specs=(any_space, any_space, any_space),
        scratch_shapes=[
            pltpu.SemaphoreType.DMA((2, rows, pieces)),
            pltpu.SemaphoreType.DMA((rows, pieces)),
            pltpu.SemaphoreType.DMA((rows, pieces)),
            pltpu.SemaphoreType.DMA((count, pieces)),
            pltpu.SemaphoreType.DMA((hops,)),
            pltpu.SemaphoreType.DMA((count,)),
            pltpu.SemaphoreType.DMA((1 + pieces,)),
        ],
        compiler_params=pltpu.CompilerParams(
            collective_id=collective_id, has_side_effects=True
        ),
        name="exchange%d" % collective_id,
    )(loc)
    return whole(mine), whole(other)


def reduce_kernel(
    rows, cols, auxs, groups, amps, b_col, fock, total, diag, part, landed, held,
    psend, precv, dsend, drecv, lsem, tsem,
):
    row, col, aux = lax.axis_index("row"), lax.axis_index("col"), lax.axis_index("aux")
    count = cols * auxs
    me = col * auxs + aux
    height, width = total.shape
    size = height // groups
    tile = min(size, 256)

    def fetch(g):
        return pltpu.make_async_copy(
            amps.at[pl.ds(g * size, size)], held.at[g % 2], tsem.at[g % 2]
        )

    fetch(0).start()
    meet(row, col, aux, rows, cols, auxs)

    def p_copy(g, index, slot):
        return pltpu.make_async_remote_copy(
            src_ref=part.at[index, pl.ds(g * size, size)],
            dst_ref=landed.at[slot, pl.ds(g * size, size)],
            send_sem=psend.at[g, index],
            recv_sem=precv.at[g, slot],
            device_id={"col": index // auxs, "aux": lax.rem(index, auxs)},
            device_id_type=MESH,
        )

    def d_copy(p, step, own):
        piece = pl.ds(p * size, size)
        return pltpu.make_async_remote_copy(
            src_ref=fock.at[piece] if own else diag.at[piece],
            dst_ref=diag.at[piece],
            send_sem=dsend.at[(1 - step) // 2, p],
            recv_sem=drecv.at[p],
            device_id={"row": row + step},
            device_id_type=MESH,
        )

    own_diag = pltpu.make_async_copy(fock, diag, lsem.at[0])
    up, down = row < rows - 1, row > 0

    @pl.when(row == me)
    def _():
        own_diag.start()

    for p in range(groups):
        @pl.when((row == me) & up)
        def _(p=p):
            d_copy(p, 1, True).start()

        @pl.when((row == me) & down)
        def _(p=p):
            d_copy(p, -1, True).start()

    def forward(p):
        @pl.when(row > me)
        def _():
            d_copy(p, 1, False).wait_recv()

            @pl.when(up)
            def _():
                d_copy(p, 1, False).start()

        @pl.when(row < me)
        def _():
            d_copy(p, -1, False).wait_recv()

            @pl.when(down)
            def _():
                d_copy(p, -1, False).start()

    ahead = max(groups // 2, 1)
    for g in range(groups):
        if g + 1 < groups:
            fetch(g + 1).start()
        fetch(g).wait()

        @pl.loop(0, size // tile)
        def _(i, g=g):
            at = pl.ds(pl.multiple_of(i * tile, tile), tile)
            to = pl.ds(pl.multiple_of(g * size + i * tile, tile), tile)
            product = jnp.dot(
                held[g % 2, at, :], b_col[...], preferred_element_type=jnp.float32
            ).astype(part.dtype)
            for index in range(count):
                part[index, to, :] = product[:, index * width:(index + 1) * width]

        for step in range(1, count):
            p_copy(g, lax.rem(me + step, count), me).start()
        if g >= ahead:
            forward(g - ahead)
    for p in range(groups - ahead, groups):
        forward(p)

    for g in range(groups):
        for step in range(1, count):
            p_copy(g, me, lax.rem(me + step, count)).wait_recv()

        @pl.loop(0, size // tile)
        def _(i, g=g):
            at = pl.ds(pl.multiple_of(g * size + i * tile, tile), tile)
            acc = part[me, at, :].astype(jnp.float32)
            for step in range(1, count):
                index = lax.rem(me + step, count)
                acc = acc + landed[index, at, :].astype(jnp.float32)
            total[at, :] = acc.astype(total.dtype)

    for g in range(groups):
        for step in range(1, count):
            p_copy(g, lax.rem(me + step, count), me).wait_send()

    @pl.when(row == me)
    def _():
        own_diag.wait()

    for p in range(groups):
        @pl.when(up & (row >= me))
        def _(p=p):
            d_copy(p, 1, False).wait_send()

        @pl.when(down & (row <= me))
        def _(p=p):
            d_copy(p, -1, False).wait_send()


def reduce_rows(amps, b_cols, fock, sizes, collective_id):
    rows, cols, auxs = sizes
    count = cols * auxs
    height, virt = fock.shape
    across = amps.shape[1]
    width = b_cols.shape[1] // count
    groups = max(1, height // 512)
    any_space = pl.BlockSpec(memory_space=pl.ANY)
    in_vmem = pl.BlockSpec(memory_space=pltpu.VMEM)
    return pl.pallas_call(
        functools.partial(reduce_kernel, rows, cols, auxs, groups),
        out_shape=(
            jax.ShapeDtypeStruct((height, width), amps.dtype),
            jax.ShapeDtypeStruct((height, virt), fock.dtype),
        ),
        in_specs=[any_space, in_vmem, any_space],
        out_specs=(in_vmem, any_space),
        scratch_shapes=[
            pltpu.VMEM((count, height, width), amps.dtype),
            pltpu.VMEM((count, height, width), amps.dtype),
            pltpu.VMEM((2, height // groups, across), amps.dtype),
            pltpu.SemaphoreType.DMA((groups, count)),
            pltpu.SemaphoreType.DMA((groups, count)),
            pltpu.SemaphoreType.DMA((2, groups)),
            pltpu.SemaphoreType.DMA((groups,)),
            pltpu.SemaphoreType.DMA((1,)),
            pltpu.SemaphoreType.DMA((2,)),
        ],
        compiler_params=pltpu.CompilerParams(
            collective_id=collective_id, has_side_effects=True, vmem_limit_bytes=VMEM_BYTES
        ),
        name="reduce%d" % collective_id,
    )(amps, b_cols, fock)


def update_kernel(
    virt, tile, t_ref, g_row, b_row, f_row, e_row, g_col, b_col, f_col, e_col, out
):
    high, across = t_ref.shape
    contract = (((1,), (1,)), ((), ()))

    @pl.loop(0, across // tile)
    def _(j):
        base = pl.multiple_of(j * tile, tile)
        at = pl.ds(base, tile)
        acc = lax.dot_general(
            g_row[...], b_col[at, :], contract, preferred_element_type=jnp.float32
        )
        acc = acc + lax.dot_general(
            b_row[...], g_col[at, :], contract, preferred_element_type=jnp.float32
        )
        right = [
            jnp.dot(
                t_ref[:, pl.ds(pl.multiple_of(base + k * virt, virt), virt)],
                f_col[pl.ds(pl.multiple_of(base + k * virt, virt), virt), :],
                preferred_element_type=jnp.float32,
            )
            for k in range(tile // virt)
        ]
        left = [
            lax.dot_general(
                f_row[k * virt:(k + 1) * virt, :],
                t_ref[k * virt:(k + 1) * virt, at],
                (((0,), (0,)), ((), ())),
                preferred_element_type=jnp.float32,
            )
            for k in range(high // virt)
        ]
        acc = acc + jnp.concatenate(right, axis=1) + jnp.concatenate(left, axis=0)
        delta = e_row[...] + e_col[:, at]
        out[:, at] = (t_ref[:, at].astype(jnp.float32) - acc / delta).astype(out.dtype)


def update(amplitudes, g_rows, b_rows, fock, e_rows, g_cols, b_cols, diag, e_cols):
    high, across = amplitudes.shape
    virt = fock.shape[1]
    aux = b_rows.shape[1]
    row_tile, col_tile = min(ROW_TILE, high), min(COL_TILE, across)
    by_row = lambda i: (i, 0)
    fixed = lambda i: (0, 0)
    return pl.pallas_call(
        functools.partial(update_kernel, virt, col_tile),
        out_shape=jax.ShapeDtypeStruct(amplitudes.shape, amplitudes.dtype),
        grid=(high // row_tile,),
        in_specs=[
            pl.BlockSpec((row_tile, across), by_row),
            pl.BlockSpec((row_tile, aux), by_row),
            pl.BlockSpec((row_tile, aux), by_row),
            pl.BlockSpec((row_tile, virt), by_row),
            pl.BlockSpec((row_tile, 1), by_row),
            pl.BlockSpec((across, aux), fixed),
            pl.BlockSpec((across, aux), fixed),
            pl.BlockSpec((across, virt), fixed),
            pl.BlockSpec((1, across), fixed),
        ],
        out_specs=pl.BlockSpec((row_tile, across), by_row),
        compiler_params=pltpu.CompilerParams(vmem_limit_bytes=VMEM_BYTES),
        name="update",
    )(amplitudes, g_rows, b_rows, fock, e_rows, g_cols, b_cols, diag, e_cols)


def body(sizes, amplitudes, b_factors, fock_blocks, occ_index, virt_index, eps_occ, eps_virt):
    height, across = amplitudes.shape
    b_rows, b_cols = exchange(b_factors, sizes, 0)
    g_own, diag = reduce_rows(amplitudes, b_cols, fock_blocks, sizes, 1)
    g_rows, g_cols = exchange(g_own, sizes, 2)

    def energy(start, size):
        return pair_energy(
            lax.dynamic_slice_in_dim(occ_index, start, size),
            lax.dynamic_slice_in_dim(virt_index, start, size),
            eps_occ,
            eps_virt,
        )

    e_rows = energy(lax.axis_index("row") * height, height)
    e_cols = energy(lax.axis_index(("col", "aux")) * across, across)
    return update(
        amplitudes, g_rows, b_rows, fock_blocks, e_rows[:, None],
        g_cols, b_cols, diag, e_cols[None, :],
    )


def solution(mesh):
    in_specs = (
        P(("groups", "row"), ("col", "aux")),
        P(("groups", "row"), ("col", "aux")),
        P(("groups", "row"), None),
        P("groups"),
        P("groups"),
        P("groups"),
        P("groups"),
    )
    out_specs = P(("groups", "row"), ("col", "aux"))
    sizes = (mesh.shape["row"], mesh.shape["col"], mesh.shape["aux"])
    return jax.shard_map(
        functools.partial(body, sizes),
        mesh=mesh, in_specs=in_specs, out_specs=out_specs, check_vma=False,
    )
```

```python
import functools

import jax
import jax.numpy as jnp
from jax import lax
from jax.experimental import pallas as pl
from jax.experimental.pallas import tpu as pltpu
from jax.sharding import PartitionSpec as P

MESH = pl.DeviceIdType.MESH
LANES = 128
ROW_TILE = 512
COL_TILE = 1024
VMEM_BYTES = 60 * 1024 * 1024


def pair_energy(occ_part, virt_part, eps_occ, eps_virt):
    virt_hit = virt_part[:, None] == jnp.arange(eps_virt.shape[0], dtype=jnp.int32)[None, :]
    occ_hit = occ_part[:, None] == jnp.arange(eps_occ.shape[0], dtype=jnp.int32)[None, :]
    upper = jnp.sum(jnp.where(virt_hit, eps_virt[None, :], 0.0), axis=1)
    lower = jnp.sum(jnp.where(occ_hit, eps_occ[None, :], 0.0), axis=1)
    return upper - lower


def slab(ref, index, width, start, size):
    if width % LANES == 0:
        return ref.at[pl.ds(start, size), pl.ds(pl.multiple_of(index * width, LANES), width)]
    return ref.at[index, pl.ds(start, size)]


def slab_shape(count, rows, width):
    return (rows, count * width) if width % LANES == 0 else (count, rows, width)


def whole(array):
    if array.ndim == 2:
        return array
    count, rows, width = array.shape
    return array.transpose(1, 0, 2).reshape(rows, count * width)


def meet(row, col, aux, rows, cols, auxs):
    barrier = pltpu.get_barrier_semaphore()

    def greet(device):
        pl.semaphore_signal(barrier, inc=1, device_id=device, device_id_type=MESH)

    @pl.when(row > 0)
    def _():
        greet({"row": row - 1})

    @pl.when(row < rows - 1)
    def _():
        greet({"row": row + 1})

    for step in range(1, cols * auxs):
        other = lax.rem(col * auxs + aux + step, cols * auxs)
        greet({"col": other // auxs, "aux": lax.rem(other, auxs)})
    above = jnp.where(row > 0, 1, 0)
    below = jnp.where(row < rows - 1, 1, 0)
    pl.semaphore_wait(barrier, cols * auxs - 1 + above + below)


def exchange_kernel(
    rows, cols, auxs, pieces, loc, along, mine, other,
    zsend, zrecv, csend, crecv, rsend, rrecv, lsem,
):
    row, col, aux = lax.axis_index("row"), lax.axis_index("col"), lax.axis_index("aux")
    count = cols * auxs
    me = col * auxs + aux
    height, width = loc.shape
    size = height // pieces
    meet(row, col, aux, rows, cols, auxs)

    def held(k, p, own):
        return loc.at[pl.ds(p * size, size)] if own else along.at[k, pl.ds(p * size, size)]

    def z_copy(k, p, step, own=False):
        return pltpu.make_async_remote_copy(
            src_ref=held(k, p, own),
            dst_ref=along.at[k, pl.ds(p * size, size)],
            send_sem=zsend.at[(1 - step) // 2, k, p],
            recv_sem=zrecv.at[k, p],
            device_id={"row": row + step},
            device_id_type=MESH,
        )

    def c_copy(k, p, slot, own=False):
        return pltpu.make_async_remote_copy(
            src_ref=held(k, p, own),
            dst_ref=slab(other, slot, width, p * size, size),
            send_sem=csend.at[k, p],
            recv_sem=crecv.at[slot, p],
            device_id={"col": k // auxs, "aux": lax.rem(k, auxs)},
            device_id_type=MESH,
        )

    def c_local(k, p, own=False):
        return pltpu.make_async_copy(
            held(k, p, own), slab(other, me, width, p * size, size), lsem.at[1 + p]
        )

    def dispatch(k, p, own=False):
        @pl.when(k != me)
        def _():
            c_copy(k, p, me, own).start()

        @pl.when(k == me)
        def _():
            c_local(k, p, own).start()

    def r_copy(index, to_col, to_aux, hop, own):
        return pltpu.make_async_remote_copy(
            src_ref=loc if own else slab(mine, index, width, 0, height),
            dst_ref=slab(mine, index, width, 0, height),
            send_sem=rsend.at[hop],
            recv_sem=rrecv.at[index],
            device_id={"col": to_col, "aux": to_aux},
            device_id_type=MESH,
        )

    def r_sends():
        first, second = [], []
        for step in range(1, cols):
            first.append(r_copy(me, lax.rem(col + step, cols), aux, step - 1, True))
        hop = cols - 1
        for step in range(cols):
            from_col = lax.rem(col + step, cols)
            for turn in range(1, auxs):
                second.append((
                    from_col * auxs + aux,
                    r_copy(from_col * auxs + aux, col, lax.rem(aux + turn, auxs), hop, step == 0),
                ))
                hop += 1
        return first, second

    first, second = r_sends()
    for copy in first:
        copy.start()
    for _, copy in second[: auxs - 1]:
        copy.start()
    for p in range(pieces):
        @pl.when(row < rows - 1)
        def _(p=p):
            z_copy(row, p, 1, True).start()

        @pl.when(row > 0)
        def _(p=p):
            z_copy(row, p, -1, True).start()

        dispatch(row, p, True)
    local = pltpu.make_async_copy(loc, slab(mine, me, width, 0, height), lsem.at[0])
    local.start()

    for s in range(1, rows):
        for p in range(pieces):
            @pl.when(row - s >= 0)
            def _(s=s, p=p):
                k = row - s
                z_copy(k, p, 1).wait_recv()

                @pl.when(row < rows - 1)
                def _():
                    z_copy(k, p, 1).start()

                dispatch(k, p)

            @pl.when(row + s < rows)
            def _(s=s, p=p):
                k = row + s
                z_copy(k, p, -1).wait_recv()

                @pl.when(row > 0)
                def _():
                    z_copy(k, p, -1).start()

                dispatch(k, p)
        if s == max(1, rows - 2):
            for index, copy in second[auxs - 1:]:
                r_copy(index, col, aux, 0, False).wait_recv()
                copy.start()

    for step in range(cols):
        from_col = lax.rem(col + step, cols)
        for turn in range(1, auxs):
            index = from_col * auxs + lax.rem(aux + turn, auxs)
            r_copy(index, col, aux, 0, False).wait_recv()
    for copy in first:
        copy.wait_send()
    for _, copy in second:
        copy.wait_send()
    local.wait()
    for step in range(1, count):
        index = lax.rem(me + step, count)
        for p in range(pieces):
            c_copy(me, p, index).wait_recv()
    for k in range(rows):
        for p in range(pieces):
            @pl.when(k != me)
            def _(k=k, p=p):
                c_copy(k, p, me).wait_send()

            @pl.when(k == me)
            def _(k=k, p=p):
                c_local(k, p).wait()

            @pl.when((row < rows - 1) & (row >= k))
            def _(k=k, p=p):
                z_copy(k, p, 1).wait_send()

            @pl.when((row > 0) & (row <= k))
            def _(k=k, p=p):
                z_copy(k, p, -1).wait_send()


def exchange(loc, sizes, collective_id):
    rows, cols, auxs = sizes
    count = cols * auxs
    height, width = loc.shape
    pieces = max(1, 32 // rows)
    shape = slab_shape(count, height, width)
    hops = cols - 1 + cols * (auxs - 1)
    any_space = pl.BlockSpec(memory_space=pl.ANY)
    _, mine, other = pl.pallas_call(
        functools.partial(exchange_kernel, rows, cols, auxs, pieces),
        out_shape=(
            jax.ShapeDtypeStruct((rows, height, width), loc.dtype),
            jax.ShapeDtypeStruct(shape, loc.dtype),
            jax.ShapeDtypeStruct(shape, loc.dtype),
        ),
        in_specs=[any_space],
        out_specs=(any_space, any_space, any_space),
        scratch_shapes=[
            pltpu.SemaphoreType.DMA((2, rows, pieces)),
            pltpu.SemaphoreType.DMA((rows, pieces)),
            pltpu.SemaphoreType.DMA((rows, pieces)),
            pltpu.SemaphoreType.DMA((count, pieces)),
            pltpu.SemaphoreType.DMA((hops,)),
            pltpu.SemaphoreType.DMA((count,)),
            pltpu.SemaphoreType.DMA((1 + pieces,)),
        ],
        compiler_params=pltpu.CompilerParams(
            collective_id=collective_id, has_side_effects=True
        ),
        name="exchange%d" % collective_id,
    )(loc)
    return whole(mine), whole(other)


def reduce_kernel(
    rows, cols, auxs, groups, amps, b_col, fock, total, diag, part, landed, held,
    psend, precv, dsend, drecv, lsem, tsem,
):
    row, col, aux = lax.axis_index("row"), lax.axis_index("col"), lax.axis_index("aux")
    count = cols * auxs
    me = col * auxs + aux
    height, width = total.shape
    size = height // groups
    tile = min(size, 256)

    def fetch(g):
        return pltpu.make_async_copy(
            amps.at[pl.ds(g * size, size)], held.at[g % 2], tsem.at[g % 2]
        )

    fetch(0).start()
    meet(row, col, aux, rows, cols, auxs)

    def p_copy(g, index, slot):
        return pltpu.make_async_remote_copy(
            src_ref=part.at[index, pl.ds(g * size, size)],
            dst_ref=landed.at[slot, pl.ds(g * size, size)],
            send_sem=psend.at[g, index],
            recv_sem=precv.at[g, slot],
            device_id={"col": index // auxs, "aux": lax.rem(index, auxs)},
            device_id_type=MESH,
        )

    def d_copy(p, step, own):
        piece = pl.ds(p * size, size)
        return pltpu.make_async_remote_copy(
            src_ref=fock.at[piece] if own else diag.at[piece],
            dst_ref=diag.at[piece],
            send_sem=dsend.at[(1 - step) // 2, p],
            recv_sem=drecv.at[p],
            device_id={"row": row + step},
            device_id_type=MESH,
        )

    own_diag = pltpu.make_async_copy(fock, diag, lsem.at[0])
    up, down = row < rows - 1, row > 0

    @pl.when(row == me)
    def _():
        own_diag.start()

    for p in range(groups):
        @pl.when((row == me) & up)
        def _(p=p):
            d_copy(p, 1, True).start()

        @pl.when((row == me) & down)
        def _(p=p):
            d_copy(p, -1, True).start()

    def forward(p):
        @pl.when(row > me)
        def _():
            d_copy(p, 1, False).wait_recv()

            @pl.when(up)
            def _():
                d_copy(p, 1, False).start()

        @pl.when(row < me)
        def _():
            d_copy(p, -1, False).wait_recv()

            @pl.when(down)
            def _():
                d_copy(p, -1, False).start()

    ahead = max(groups // 2, 1)
    for g in range(groups):
        if g + 1 < groups:
            fetch(g + 1).start()
        fetch(g).wait()

        @pl.loop(0, size // tile)
        def _(i, g=g):
            at = pl.ds(pl.multiple_of(i * tile, tile), tile)
            to = pl.ds(pl.multiple_of(g * size + i * tile, tile), tile)
            product = jnp.dot(
                held[g % 2, at, :], b_col[...], preferred_element_type=jnp.float32
            ).astype(part.dtype)
            for index in range(count):
                part[index, to, :] = product[:, index * width:(index + 1) * width]

        for step in range(1, count):
            p_copy(g, lax.rem(me + step, count), me).start()
        if g >= ahead:
            forward(g - ahead)
    for p in range(groups - ahead, groups):
        forward(p)

    for g in range(groups):
        for step in range(1, count):
            p_copy(g, me, lax.rem(me + step, count)).wait_recv()

        @pl.loop(0, size // tile)
        def _(i, g=g):
            at = pl.ds(pl.multiple_of(g * size + i * tile, tile), tile)
            acc = part[me, at, :].astype(jnp.float32)
            for step in range(1, count):
                index = lax.rem(me + step, count)
                acc = acc + landed[index, at, :].astype(jnp.float32)
            total[at, :] = acc.astype(total.dtype)

    for g in range(groups):
        for step in range(1, count):
            p_copy(g, lax.rem(me + step, count), me).wait_send()

    @pl.when(row == me)
    def _():
        own_diag.wait()

    for p in range(groups):
        @pl.when(up & (row >= me))
        def _(p=p):
            d_copy(p, 1, False).wait_send()

        @pl.when(down & (row <= me))
        def _(p=p):
            d_copy(p, -1, False).wait_send()


def reduce_rows(amps, b_cols, fock, sizes, collective_id):
    rows, cols, auxs = sizes
    count = cols * auxs
    height, virt = fock.shape
    across = amps.shape[1]
    width = b_cols.shape[1] // count
    groups = max(1, height // 512)
    any_space = pl.BlockSpec(memory_space=pl.ANY)
    in_vmem = pl.BlockSpec(memory_space=pltpu.VMEM)
    return pl.pallas_call(
        functools.partial(reduce_kernel, rows, cols, auxs, groups),
        out_shape=(
            jax.ShapeDtypeStruct((height, width), amps.dtype),
            jax.ShapeDtypeStruct((height, virt), fock.dtype),
        ),
        in_specs=[any_space, in_vmem, any_space],
        out_specs=(in_vmem, any_space),
        scratch_shapes=[
            pltpu.VMEM((count, height, width), amps.dtype),
            pltpu.VMEM((count, height, width), amps.dtype),
            pltpu.VMEM((2, height // groups, across), amps.dtype),
            pltpu.SemaphoreType.DMA((groups, count)),
            pltpu.SemaphoreType.DMA((groups, count)),
            pltpu.SemaphoreType.DMA((2, groups)),
            pltpu.SemaphoreType.DMA((groups,)),
            pltpu.SemaphoreType.DMA((1,)),
            pltpu.SemaphoreType.DMA((2,)),
        ],
        compiler_params=pltpu.CompilerParams(
            collective_id=collective_id, has_side_effects=True, vmem_limit_bytes=VMEM_BYTES
        ),
        name="reduce%d" % collective_id,
    )(amps, b_cols, fock)


def update_kernel(
    virt, tile, t_ref, g_row, b_row, f_row, e_row, g_col, b_col, f_col, e_col, out
):
    high, across = t_ref.shape
    contract = (((1,), (1,)), ((), ()))

    @pl.loop(0, across // tile)
    def _(j):
        base = pl.multiple_of(j * tile, tile)
        at = pl.ds(base, tile)
        acc = lax.dot_general(
            g_row[...], b_col[at, :], contract, preferred_element_type=jnp.float32
        )
        acc = acc + lax.dot_general(
            b_row[...], g_col[at, :], contract, preferred_element_type=jnp.float32
        )
        right = [
            jnp.dot(
                t_ref[:, pl.ds(pl.multiple_of(base + k * virt, virt), virt)],
                f_col[pl.ds(pl.multiple_of(base + k * virt, virt), virt), :],
                preferred_element_type=jnp.float32,
            )
            for k in range(tile // virt)
        ]
        left = [
            lax.dot_general(
                f_row[k * virt:(k + 1) * virt, :],
                t_ref[k * virt:(k + 1) * virt, at],
                (((0,), (0,)), ((), ())),
                preferred_element_type=jnp.float32,
            )
            for k in range(high // virt)
        ]
        acc = acc + jnp.concatenate(right, axis=1) + jnp.concatenate(left, axis=0)
        delta = e_row[...] + e_col[:, at]
        out[:, at] = (t_ref[:, at].astype(jnp.float32) - acc / delta).astype(out.dtype)


def update(amplitudes, g_rows, b_rows, fock, e_rows, g_cols, b_cols, diag, e_cols):
    high, across = amplitudes.shape
    virt = fock.shape[1]
    aux = b_rows.shape[1]
    row_tile, col_tile = min(ROW_TILE, high), min(COL_TILE, across)
    by_row = lambda i: (i, 0)
    fixed = lambda i: (0, 0)
    return pl.pallas_call(
        functools.partial(update_kernel, virt, col_tile),
        out_shape=jax.ShapeDtypeStruct(amplitudes.shape, amplitudes.dtype),
        grid=(high // row_tile,),
        in_specs=[
            pl.BlockSpec((row_tile, across), by_row),
            pl.BlockSpec((row_tile, aux), by_row),
            pl.BlockSpec((row_tile, aux), by_row),
            pl.BlockSpec((row_tile, virt), by_row),
            pl.BlockSpec((row_tile, 1), by_row),
            pl.BlockSpec((across, aux), fixed),
            pl.BlockSpec((across, aux), fixed),
            pl.BlockSpec((across, virt), fixed),
            pl.BlockSpec((1, across), fixed),
        ],
        out_specs=pl.BlockSpec((row_tile, across), by_row),
        compiler_params=pltpu.CompilerParams(vmem_limit_bytes=VMEM_BYTES),
        name="update",
    )(amplitudes, g_rows, b_rows, fock, e_rows, g_cols, b_cols, diag, e_cols)


def body(sizes, amplitudes, b_factors, fock_blocks, occ_index, virt_index, eps_occ, eps_virt):
    height, across = amplitudes.shape
    b_rows, b_cols = exchange(b_factors, sizes, 0)
    g_own, diag = reduce_rows(amplitudes, b_cols, fock_blocks, sizes, 1)
    g_rows, g_cols = exchange(g_own, sizes, 2)

    def energy(start, size):
        return pair_energy(
            lax.dynamic_slice_in_dim(occ_index, start, size),
            lax.dynamic_slice_in_dim(virt_index, start, size),
            eps_occ,
            eps_virt,
        )

    e_rows = energy(lax.axis_index("row") * height, height)
    e_cols = energy(lax.axis_index(("col", "aux")) * across, across)
    return update(
        amplitudes, g_rows, b_rows, fock_blocks, e_rows[:, None],
        g_cols, b_cols, diag, e_cols[None, :],
    )


def solution(mesh):
    in_specs = (
        P(("groups", "row"), ("col", "aux")),
        P(("groups", "row"), ("col", "aux")),
        P(("groups", "row"), None),
        P("groups"),
        P("groups"),
        P("groups"),
        P("groups"),
    )
    out_specs = P(("groups", "row"), ("col", "aux"))
    sizes = (mesh.shape["row"], mesh.shape["col"], mesh.shape["aux"])
    return jax.shard_map(
        functools.partial(body, sizes),
        mesh=mesh, in_specs=in_specs, out_specs=out_specs, check_vma=False,
    )
```
